32 devices in a mesh: groups: 2 (over y), space: 4 (over z), wave: 4 (over x, core).
Axes of the slice: x: 2, y: 2, z: 4, core: 2. Of those that a mesh axis runs over, the one named last changes fastest.
Arguments:
- density: float32 [512, 16, 128], P(('groups', 'space')), parts along dimension 0, may hold values from -6 to 6
- even_taps: float32 [15], replicated, may hold values from -1.5 to 1.5
- odd_taps: float32 [15], replicated, may hold values from -1.5 to 1.5
- low_taps: float32 [15], replicated, may hold values from -1.5 to 1.5
- wavelets: int32 [40, 2], replicated, may hold values from 0 to 2, as said below
- pairs: int32 [32, 2], replicated, may hold values from -1 to 39, as said below
Outputs:
- second: float32 [32, 256, 8, 64], P('wave', ('groups', 'space')), parts along dimension 1
The draws below stay inside these ranges and needn't reach their ends.
There are 2 independent parts, one for each index of `groups`. The reference program is written for one: setup_inputs(seed, part) draws one part's arguments, and reference() takes and returns one part's arrays. A program takes and returns all parts, laid end to end along the dimension named above; an argument that names none is the same for every part. Nothing has to cross between parts.
Inputs may be any that keep to these rules, and one draw needn't show every extreme that they name: `wavelets`: column 0 is a dilation level below 3, column 1 an orientation 0, 1 or 2. Rows below 5 have levels below 2; the last row has level 2. `pairs`: the slots form aligned blocks of 8 rows, one block for each index of wave. In every block the live rows come first and at least one is live; some block has all 8 rows live. A live row holds a first-order field below 5 and a wavelet row of 5 or more whose level is above that field's level; a dead row is (-1, 0).
All inputs are finite; a program needn't handle non-finite values.
Results may differ from the reference program's by a relative error of at most 0.0003.
Values sent between devices are 32-bit elements; how exact they have to be, the bound alone decides.
A program may use at most 64 MiB of HBM per device.

```python
import jax
import jax.numpy as jnp
from jax import lax

NY = 16
NZ = 128
PAIR_DEV = 8
NFIRST = 5
NWAVE = 40
TAPS = 15
LEVELS = 3
REACH = 28
NX = 256
PAIRS = 32


def wavelet_table(key):
    first_levels = jax.random.randint(jax.random.fold_in(key, 11), (NWAVE,), 0, LEVELS - 1)
    other_levels = jax.random.randint(jax.random.fold_in(key, 16), (NWAVE,), 0, LEVELS)
    rows = jnp.arange(NWAVE)
    level_draw = jnp.where(rows < NFIRST, first_levels, other_levels)
    orient_draw = jax.random.randint(jax.random.fold_in(key, 12), (NWAVE,), 0, 3)
    level_draw = level_draw.at[NWAVE - 1].set(LEVELS - 1)
    orient_draw = orient_draw.at[0].set(2)
    return jnp.stack([level_draw, orient_draw], axis=1).astype(jnp.int32)


def draw_wavelets(key, part):
    return wavelet_table(key)


def draw_pairs(key, part):
    table = wavelet_table(key)
    levels = table[:, 0]
    block_count = PAIRS // PAIR_DEV
    ranking = jax.random.permutation(jax.random.fold_in(key, 13), block_count)
    heights = ranking + 1
    squared = block_count * block_count
    live_counts = jnp.maximum(1, (PAIR_DEV * heights * heights + squared - 1) // squared)
    positions = jnp.arange(PAIRS)
    slot_in_block = positions % PAIR_DEV
    block_of = positions // PAIR_DEV
    live_flags = slot_in_block < live_counts[block_of]
    field_draw = jax.random.randint(jax.random.fold_in(key, 14), (PAIRS,), 0, NFIRST)
    field_levels = levels[field_draw]
    rows = jnp.arange(NWAVE)
    eligible = (rows[None, :] >= NFIRST) & (levels[None, :] > field_levels[:, None])
    scores = jax.random.randint(jax.random.fold_in(key, 15), (PAIRS, NWAVE), 0, 1 << 20) * 64 + rows[None, :]
    scores = jnp.where(eligible, scores, -1)
    wave_draw = jnp.argmax(scores, axis=1).astype(jnp.int32)
    busiest = (ranking[block_of] == block_count - 1) & (slot_in_block == 0)
    wave_draw = jnp.where(busiest, NWAVE - 1, wave_draw)
    first_col = jnp.where(live_flags, field_draw, -1)
    second_col = jnp.where(live_flags, wave_draw, 0)
    return jnp.stack([first_col, second_col], axis=1).astype(jnp.int32)


def block_scale(key, shape, pieces, low, high):
    gain = 1.0
    for dim, shards_of in pieces:
        steps = jax.random.uniform(jax.random.fold_in(jax.random.fold_in(key, 6), dim), (shards_of,), jnp.float32, low / len(pieces), high / len(pieces))
        gain = gain * jnp.repeat(jnp.exp(steps), shape[dim] // shards_of).reshape((-1,) + (1,) * (len(shape) - 1 - dim))
    return gain


def centred(key, shape, scale, reach, shards=(), kind=jnp.bfloat16):
    result = scale * jax.random.normal(key, shape, jnp.float32)
    if shards:
        result = result * block_scale(key, shape, shards, -0.22, 0.18)
    return jnp.clip(result, -reach, reach).astype(kind)


def setup_inputs(seed: int = 0, part: int = 0) -> dict:
    key_of = jax.random.split(jax.random.key(seed), 7)
    own_keys = jax.random.split(jax.random.fold_in(key_of[6], part), 7)
    density = centred(own_keys[0], (NX, NY, NZ), 1.0, 6.0, ((0, 4),), jnp.float32)
    even_taps = centred(key_of[1], (TAPS,), TAPS ** -0.5, 1.5, (), jnp.float32)
    odd_taps = centred(key_of[2], (TAPS,), TAPS ** -0.5, 1.5, (), jnp.float32)
    low_taps = centred(key_of[3], (TAPS,), TAPS ** -0.5, 1.5, (), jnp.float32)
    wavelets = draw_wavelets(jax.random.fold_in(key_of[6], 71), part)
    pairs = draw_pairs(jax.random.fold_in(key_of[6], 71), part)
    return {"density": density, "even_taps": even_taps, "odd_taps": odd_taps, "low_taps": low_taps, "wavelets": wavelets, "pairs": pairs}


def widen(values_in, direction, margin):
    widths = [(0, 0)] * values_in.ndim
    widths[direction] = (margin, margin)
    return jnp.pad(values_in, widths)

def along(values_in, weights, dilation, direction, length_out):
    centre = weights.shape[0] // 2
    accumulated = None
    for tap_index in range(weights.shape[0]):
        offset = REACH + (tap_index - centre) * dilation
        shifted = lax.dynamic_slice_in_dim(values_in, offset, length_out, direction)
        weighted = weights[tap_index] * shifted
        accumulated = weighted if accumulated is None else accumulated + weighted
    return accumulated

def respond(values_in, level_index, orient, filters, length_out):
    even_taps, odd_taps, low_taps = filters
    dilation = jnp.left_shift(jnp.int32(1), level_index.astype(jnp.int32))

    def make_branch(band):

        def respond_oriented(source):
            signals = (source,)
            for direction in range(3):
                if direction == 0:
                    extent = length_out
                    prepared = signals
                else:
                    extent = source.shape[direction]
                    prepared = tuple((widen(signal, direction, REACH) for signal in signals))
                if direction == band:
                    signals = (along(prepared[0], even_taps, dilation, direction, extent), along(prepared[0], odd_taps, dilation, direction, extent))
                else:
                    signals = tuple((along(signal, low_taps, dilation, direction, extent) for signal in prepared))
            real_part, imag_part = signals
            return jnp.sqrt(real_part * real_part + imag_part * imag_part + 1e-06)
        return respond_oriented
    return lax.switch(orient.astype(jnp.int32), [make_branch(0), make_branch(1), make_branch(2)], values_in)

def reference(density, even_taps, odd_taps, low_taps, wavelets, pairs):
    filters = (even_taps, odd_taps, low_taps)
    wide_density = widen(density, 0, REACH)
    firsts = jnp.stack([respond(wide_density, wavelets[field_index, 0], wavelets[field_index, 1], filters, NX) for field_index in range(NFIRST)])
    first_wide = widen(firsts, 1, REACH)

    def one_pair(pair_row):
        source = lax.dynamic_index_in_dim(first_wide, jnp.maximum(pair_row[0], 0), 0, keepdims=False)

        def work_pair(values_in):
            level_index = wavelets[pair_row[1], 0]
            orient = wavelets[pair_row[1], 1]
            return respond(values_in, level_index, orient, filters, NX)[::2, ::2, ::2]

        def skip_pair(values_in):
            return jnp.zeros((NX // 2, NY // 2, NZ // 2), values_in.dtype)
        return lax.cond(pair_row[0] >= 0, work_pair, skip_pair, source)
    return lax.map(one_pair, pairs)
```

```python
import functools

import jax
import jax.numpy as jnp
from jax import lax
from jax.experimental import pallas as pl
from jax.experimental.pallas import tpu as pltpu
from jax.sharding import PartitionSpec as P

REACH1 = 14
REACH2 = 28
HALO = REACH1 + REACH2
TAPS = 15
MID = TAPS // 2
CHUNKS = 3
KEYS = 6
FIELD_GROUP = 6
PAIR_GROUP = 8
BF = jnp.bfloat16
F32 = jnp.float32
MESH = pl.DeviceIdType.MESH


def halves(v):
    hi = v.astype(BF)
    return hi, (v - hi.astype(F32)).astype(BF)


def at(taps, t):
    return taps[t] if 0 <= t < TAPS else jnp.float32(0.0)


def build_tables(even, odd, low, zt1, zt2, wx, cy0, cyd):
    nz = zt1.shape[1] // 2
    half = nz // 2
    lane = lax.broadcasted_iota(jnp.int32, (8, nz), 1)
    sub = lax.broadcasted_iota(jnp.int32, (8, nz), 0)
    left = lane < half

    def split(t):
        return jnp.where(left, at(even, t), at(odd, t))

    def plain(t):
        return jnp.full((8, nz), at(low, t), F32)

    kinds = (plain, split)
    for n, kind in enumerate(kinds):
        for t in range(TAPS):
            wx[n * TAPS + t] = kind(t)
        for par in range(2):
            for s in range(8):
                k = par - 2 * s
                cy0[(n * 2 + par) * 8 + s] = jnp.where(sub >= s, kind(MID + k), kind(MID + 16 + k))
        for delta in (1, 2):
            for s in range(8):
                slot = ((delta - 1) * 2 + n) * 8 + s
                if s % delta:
                    cyd[slot] = jnp.zeros((8, nz), F32)
                else:
                    k = -s // delta
                    cyd[slot] = jnp.where(sub >= s, kind(MID + k), kind(MID + 8 // delta + k))

    blk = 32
    row = lax.broadcasted_iota(jnp.int32, (blk, nz), 0)
    col = lax.broadcasted_iota(jnp.int32, (blk, nz), 1)
    wide = jnp.where(col < half, col, col - half)
    is_left = col < half

    def bands(diff, step):
        lo = jnp.zeros((blk, nz), F32)
        eo = jnp.zeros((blk, nz), F32)
        for t in range(TAPS):
            hit = diff == (t - MID) * step
            lo = jnp.where(hit, low[t], lo)
            eo = jnp.where(hit, jnp.where(is_left, even[t], odd[t]), eo)
        return lo, eo

    for level in (0, 1):
        for r0 in range(0, nz, blk):
            for n, v in enumerate(bands(row + r0 - 2 * wide, 1 << level)):
                hi, lo = halves(v)
                ref = zt1.at[level * 2 + n]
                ref[pl.ds(r0, blk), pl.ds(0, nz)] = hi
                ref[pl.ds(r0, blk), pl.ds(nz, nz)] = lo
                ref[pl.ds(nz + r0, blk), pl.ds(0, nz)] = hi
                ref[pl.ds(nz + r0, blk), pl.ds(nz, nz)] = jnp.zeros_like(lo)
    for delta in (1, 2):
        for r0 in range(0, half, blk):
            for n, v in enumerate(bands(row + r0 - wide, delta)):
                hi, lo = halves(v)
                ref = zt2.at[(delta - 1) * 2 + n]
                ref[pl.ds(r0, blk)] = hi
                ref[pl.ds(half + r0, blk)] = hi
                ref[pl.ds(2 * half + r0, blk)] = lo
                ref[pl.ds(3 * half + r0, blk)] = jnp.zeros_like(lo)


def exchange(ny, even, odd, low, density, before, after, zt1, zt2, wx, cy0, cyd, zsend, zrecv, psend, precv):
    rows = density.shape[0]
    halo = HALO * ny
    part = halo // 2
    chunk = part // CHUNKS
    count = lax.axis_size("space")
    space = lax.axis_index("space")
    wave = lax.axis_index("wave")
    core = lax.rem(wave, 2)
    partner = wave + 1 - 2 * core
    above = space < count - 1
    below = space > 0
    barrier = pltpu.get_barrier_semaphore()

    @pl.when(above)
    def _():
        pl.semaphore_signal(barrier, 1, device_id={"space": space + 1}, device_id_type=MESH)

    @pl.when(below)
    def _():
        pl.semaphore_signal(barrier, 1, device_id={"space": space - 1}, device_id_type=MESH)

    pl.semaphore_signal(barrier, 1, device_id={"wave": partner}, device_id_type=MESH)
    peers = 1 + above.astype(jnp.int32) + below.astype(jnp.int32)
    pl.semaphore_wait(barrier, peers)

    landing = (before, after)
    sends = (above, below)
    arrives = (below, above)

    def zcopy(way, q):
        r = core * part + q * chunk
        return pltpu.make_async_remote_copy(
            src_ref=density.at[pl.ds(r + (rows - halo if way == 0 else 0), chunk)],
            dst_ref=landing[way].at[pl.ds(r, chunk)],
            send_sem=zsend.at[way, q],
            recv_sem=zrecv.at[way, q],
            device_id={"space": space + 1 if way == 0 else space - 1},
            device_id_type=MESH,
        )

    def pcopy(way, q, first):
        piece = landing[way].at[pl.ds(first * part + q * chunk, chunk)]
        return pltpu.make_async_remote_copy(
            src_ref=piece,
            dst_ref=piece,
            send_sem=psend.at[way, q],
            recv_sem=precv.at[way, q],
            device_id={"wave": partner},
            device_id_type=MESH,
        )

    every = [(way, q) for q in range(CHUNKS) for way in range(2)]
    for way, q in every:

        @pl.when(sends[way])
        def _():
            zcopy(way, q).start()

    build_tables(even, odd, low, zt1, zt2, wx, cy0, cyd)
    for way, q in every:

        @pl.when(arrives[way])
        def _():
            zcopy(way, q).wait_recv()
            pcopy(way, q, core).start()

    for way, q in every:

        @pl.when(sends[way])
        def _():
            zcopy(way, q).wait_send()

        @pl.when(arrives[way])
        def _():
            pcopy(way, q, core).wait_send()
            pcopy(way, q, 1 - core).wait_recv()


def dot(a, b):
    return jnp.dot(a, b, preferred_element_type=F32)


def magnitude(v):
    sq = v * v
    a = sq + pltpu.roll(sq, v.shape[1] // 2, 1) + 1e-06
    return a * lax.rsqrt(a)


def turned(planes, coeffs):
    total = None
    for v, c in zip(planes, coeffs):
        for s in range(8):
            term = c[s] * (v if s == 0 else pltpu.roll(v, s, 0))
            total = term if total is None else total + term
    return total


def kernel(ny, wav, pairs, before, centre, after, zt1, zt2, wx, cy0, cyd, out, ext, hl, zp0, zp1, eb, u, flags, sems):
    nz = ext.shape[1]
    halo = HALO * ny
    rows = centre.shape[0] // ny
    per_dev = out.shape[0]
    spots = rows // 2 + REACH2
    pad = REACH2 // 2
    slots = rows // 2 + HALO
    space = lax.axis_index("space")
    last = lax.axis_size("space") - 1
    start = lax.axis_index("wave") * per_dev
    inner = pltpu.make_async_copy(centre, ext.at[pl.ds(halo, rows * ny)], sems.at[1])
    inner.start()
    edges = (
        (space > 0, pltpu.make_async_copy(before, ext.at[pl.ds(0, halo)], sems.at[0]), 0),
        (space < last, pltpu.make_async_copy(after, ext.at[pl.ds(halo + rows * ny, halo)], sems.at[2]), halo + rows * ny),
    )
    for there, copy, where in edges:

        @pl.when(there)
        def _():
            copy.start()

        @pl.when(jnp.logical_not(there))
        def _():
            ext[pl.ds(where, halo)] = jnp.zeros((halo, nz), F32)

    def key_of(f):
        return wav[0, f] * 3 + wav[1, f]

    for k in range(KEYS + 1):
        flags[k] = 0
    for p in range(per_dev):
        f = pairs[0, start + p]
        flags[jnp.where(f < 0, KEYS, key_of(jnp.maximum(f, 0)))] = 1

    for there, copy, _ in edges:

        @pl.when(there)
        def _():
            copy.wait()

    inner.wait()

    def split_rows(c, carry):
        for ypar in range(2):
            v = ext[pl.ds(c * 4 * ny + ypar, 32, stride=2), :]
            hi, lo = halves(v.reshape(2, 2, 8, nz))
            for xpar in range(2):
                both = jnp.concatenate([hi[:, xpar].reshape(16, nz), lo[:, xpar].reshape(16, nz)], axis=1)
                hl[xpar * 2 + ypar, c] = both
        return carry

    lax.fori_loop(0, slots // 2, split_rows, 0)

    def folded(r):
        return r[:, :nz] + r[:, nz:]

    blocks0 = (slots - 6) // 2
    first_block = 1
    for n in range(2):
        need = flags[2] if n else flags[0] + flags[1]

        @pl.when(need > 0)
        def _():
            def zpass(q, carry):
                lhs = hl[q, pl.ds(first_block, blocks0)].reshape(blocks0 * 16, 2 * nz)
                r = folded(dot(lhs, zt1[n]))
                zp0[n * 4 + q, pl.ds(2 * first_block, 2 * blocks0)] = r.reshape(2 * blocks0, 8, nz)
                return carry

            lax.fori_loop(0, 4, zpass, 0)

        need = flags[5] if n else flags[3] + flags[4]

        @pl.when(need > 0)
        def _():
            r = folded(dot(hl[0].reshape(slots * 8, 2 * nz), zt1[2 + n]))
            zp1[n] = r.reshape(slots, 8, nz)

    def store_field(key, c, mags):
        v = jnp.concatenate(mags, axis=0)
        hi, lo = halves(v)
        lane = lax.broadcasted_iota(jnp.int32, v.shape, 1)
        low_part = (v - hi.astype(F32))
        mixed = jnp.where(lane < nz // 2, v, low_part).astype(BF)
        both = jnp.concatenate([mixed, hi], axis=1)
        eb[key, pl.ds(c * (FIELD_GROUP // 2), FIELD_GROUP // 2)] = both.reshape(FIELD_GROUP // 2, 16, 2 * nz)

    def kinds(o):
        return (o == 0).astype(jnp.int32), (o == 1).astype(jnp.int32), (o == 2).astype(jnp.int32)

    def level0(o, carry):
        @pl.when(flags[o] > 0)
        def _():
            kx, ky, kz = kinds(o)

            def group(c, inner_carry):
                i = c * FIELD_GROUP
                accs = [[None, None] for _ in range(FIELD_GROUP)]
                for t in range(TAPS):
                    w = wx[kx * TAPS + t]
                    xpar = (t + 1) % 2
                    j = (t + MID) // 2
                    for par in range(2):
                        src = kz * 4 + xpar * 2 + par
                        for g in range(FIELD_GROUP):
                            term = w * zp0[src, i + g + j]
                            accs[g][par] = term if t == 0 else accs[g][par] + term
                coeffs = [[cy0[(ky * 2 + par) * 8 + s] for s in range(8)] for par in range(2)]
                store_field(o, c, [magnitude(turned(a, coeffs)) for a in accs])
                return inner_carry

            lax.fori_loop(0, spots // FIELD_GROUP, group, 0)

        return carry

    lax.fori_loop(0, 3, level0, 0)

    def level1(o, carry):
        @pl.when(flags[3 + o] > 0)
        def _():
            kx, ky, kz = kinds(o)

            def group(c, inner_carry):
                i = c * FIELD_GROUP
                accs = [None] * FIELD_GROUP
                for t in range(TAPS):
                    w = wx[kx * TAPS + t]
                    for g in range(FIELD_GROUP):
                        term = w * zp1[kz, i + g + t]
                        accs[g] = term if t == 0 else accs[g] + term
                coeffs = [[cyd[ky * 8 + s] for s in range(8)]]
                store_field(3 + o, c, [magnitude(turned([a], coeffs)) for a in accs])
                return inner_carry

            lax.fori_loop(0, spots // FIELD_GROUP, group, 0)

        return carry

    lax.fori_loop(0, 3, level1, 0)

    edge = pad // 2

    @pl.when(space == 0)
    def _():
        for k in range(KEYS):
            eb[k, pl.ds(0, edge)] = jnp.zeros((edge, 16, 2 * nz), BF)

    @pl.when(space == last)
    def _():
        for k in range(KEYS):
            eb[k, pl.ds(spots // 2 - edge, edge)] = jnp.zeros((edge, 16, 2 * nz), BF)

    def do_pair(p, carry):
        f = pairs[0, start + p]
        w = pairs[1, start + p]

        @pl.when(f >= 0)
        def _():
            o = wav[1, w]
            step = wav[0, w]
            kx, ky, kz = kinds(o)
            lhs = eb[key_of(f)].reshape(spots * 8, 2 * nz)
            u[...] = dot(lhs, zt2[(step - 1) * 2 + kz]).reshape(spots, 8, nz)
            coeffs = [[cyd[((step - 1) * 2 + ky) * 8 + s] for s in range(8)]]
            for g0 in range(0, rows // 2, PAIR_GROUP):
                accs = [None] * PAIR_GROUP
                for t in range(TAPS):
                    weight = wx[kx * TAPS + t]
                    base = pad + g0 + (t - MID) * step
                    for g in range(PAIR_GROUP):
                        term = weight * u[base + g]
                        accs[g] = term if t == 0 else accs[g] + term
                for g in range(PAIR_GROUP):
                    out[p, g0 + g] = magnitude(turned([accs[g]], coeffs))[:, : nz // 2]

        @pl.when(f < 0)
        def _():
            out[p] = jnp.zeros(out.shape[1:], F32)

        return carry

    lax.fori_loop(0, per_dev, do_pair, 0)


def shards(density, even_taps, odd_taps, low_taps, wavelets, pairs):
    rows, ny, nz = density.shape
    per_dev = pairs.shape[0] // lax.axis_size("wave")
    flat = density.reshape(rows * ny, nz)
    smem = pl.BlockSpec(memory_space=pltpu.SMEM)
    vmem = pl.BlockSpec(memory_space=pltpu.VMEM)
    anyw = pl.BlockSpec(memory_space=pl.ANY)
    hbm = pl.BlockSpec(memory_space=pltpu.HBM)
    halo = jax.ShapeDtypeStruct((HALO * ny, nz), F32)
    before, after, *tables = pl.pallas_call(
        functools.partial(exchange, ny),
        out_shape=(
            halo,
            halo,
            jax.ShapeDtypeStruct((4, 2 * nz, 2 * nz), BF),
            jax.ShapeDtypeStruct((4, 2 * nz, nz), BF),
            jax.ShapeDtypeStruct((2 * TAPS, 8, nz), F32),
            jax.ShapeDtypeStruct((32, 8, nz), F32),
            jax.ShapeDtypeStruct((32, 8, nz), F32),
        ),
        in_specs=[smem] * 3 + [hbm],
        out_specs=[anyw] * 2 + [vmem] * 5,
        scratch_shapes=[pltpu.SemaphoreType.DMA((2, CHUNKS))] * 4,
        compiler_params=pltpu.CompilerParams(collective_id=0, has_side_effects=True, vmem_limit_bytes=16 << 20),
        name="exchange",
    )(even_taps, odd_taps, low_taps, flat)
    slots = rows // 2 + HALO
    spots = rows // 2 + REACH2
    return pl.pallas_call(
        functools.partial(kernel, ny),
        out_shape=jax.ShapeDtypeStruct((per_dev, rows // 2, ny // 2, nz // 2), F32),
        in_specs=[smem] * 2 + [anyw, hbm, anyw] + [vmem] * 5,
        out_specs=vmem,
        scratch_shapes=[
            pltpu.VMEM(((rows + 2 * HALO) * ny, nz), F32),
            pltpu.VMEM((4, slots // 2, 16, 2 * nz), BF),
            pltpu.VMEM((8, slots, 8, nz), F32),
            pltpu.VMEM((2, slots, 8, nz), F32),
            pltpu.VMEM((KEYS, spots // 2, 16, 2 * nz), BF),
            pltpu.VMEM((spots, 8, nz), F32),
            pltpu.SMEM((KEYS + 1,), jnp.int32),
            pltpu.SemaphoreType.DMA((3,)),
        ],
        compiler_params=pltpu.CompilerParams(vmem_limit_bytes=24 << 20),
        name="scatter",
    )(wavelets.T, pairs.T, before, flat, after, *tables)


def solution(mesh):
    placed = (P(("groups", "space"), None, None), P(), P(), P(), P(), P())
    return jax.shard_map(
        shards,
        mesh=mesh,
        in_specs=placed,
        out_specs=P("wave", ("groups", "space"), None, None),
        check_vma=False,
    )
```

```python
import functools

import jax
import jax.numpy as jnp
from jax import lax
from jax.experimental import pallas as pl
from jax.experimental.pallas import tpu as pltpu
from jax.sharding import PartitionSpec as P

REACH1 = 14
REACH2 = 28
HALO = REACH1 + REACH2
TAPS = 15
MID = TAPS // 2
CHUNKS = 3
KEYS = 6
FIELD_GROUP = 6
PAIR_GROUP = 4
BLOCK = 16
WIDE = 256
LIMIT1 = 16 << 20
LIMIT2 = 24 << 20
TYPES = ((0, 2), (1, 2), (2, 0), (2, 1), (2, 2), (2, 2))
BF = jnp.bfloat16
F32 = jnp.float32
MESH = pl.DeviceIdType.MESH


def halves(v):
    hi = v.astype(BF)
    return hi, (v - hi.astype(F32)).astype(BF)


def at(taps, t):
    return taps[t] if 0 <= t < TAPS else jnp.float32(0.0)


def build_tables(even, odd, low, zt1, zt2, wx, cy0, dh, dl):
    nz = zt1.shape[1] // 2
    half = nz // 2
    lane8 = lax.broadcasted_iota(jnp.int32, (8, nz), 1)
    sub8 = lax.broadcasted_iota(jnp.int32, (8, nz), 0)

    def split(t):
        return jnp.where(lane8 < half, at(even, t), at(odd, t))

    def plain(t):
        return jnp.full((8, nz), at(low, t), F32)

    for n, kind in enumerate((plain, split)):
        for t in range(TAPS):
            wx[n * TAPS + t] = kind(t)
        for par in range(2):
            for s in range(8):
                k = par - 2 * s
                cy0[(n * 2 + par) * 8 + s] = jnp.where(sub8 >= s, kind(MID + k), kind(MID + 16 + k))

    blk = 32
    row = lax.broadcasted_iota(jnp.int32, (blk, nz), 0)
    col = lax.broadcasted_iota(jnp.int32, (blk, nz), 1)
    wide = jnp.where(col < half, col, col - half)
    is_left = col < half

    def bands(diff, step):
        lo = jnp.zeros((blk, nz), F32)
        eo = jnp.zeros((blk, nz), F32)
        for t in range(TAPS):
            hit = diff == (t - MID) * step
            lo = jnp.where(hit, low[t], lo)
            eo = jnp.where(hit, jnp.where(is_left, even[t], odd[t]), eo)
        return lo, eo

    for level in (0, 1):
        for r0 in range(0, nz, blk):
            for n, v in enumerate(bands(row + r0 - 2 * wide, 1 << level)):
                hi, lo = halves(v)
                ref = zt1.at[level * 2 + n]
                ref[pl.ds(r0, blk), pl.ds(0, nz)] = hi
                ref[pl.ds(r0, blk), pl.ds(nz, nz)] = lo
                ref[pl.ds(nz + r0, blk), pl.ds(0, nz)] = hi
                ref[pl.ds(nz + r0, blk), pl.ds(nz, nz)] = jnp.zeros_like(lo)
    for delta in (1, 2):
        for r0 in range(0, half, blk):
            for n, v in enumerate(bands(row + r0 - wide, delta)):
                hi, lo = halves(v)
                ref = zt2.at[(delta - 1) * 2 + n]
                ref[pl.ds(r0, blk)] = hi
                ref[pl.ds(half + r0, blk)] = hi
                ref[pl.ds(2 * half + r0, blk)] = lo
                ref[pl.ds(3 * half + r0, blk)] = jnp.zeros_like(lo)

    lane = lax.broadcasted_iota(jnp.int32, (8, WIDE), 1)
    xi = lane // 8
    yi = lane % 8 - lax.broadcasted_iota(jnp.int32, (8, WIDE), 0)
    sets = (even, odd, low)

    def picked(index, pairs):
        outs = [jnp.zeros((8, WIDE), F32) for _ in sets]
        for value, t in pairs:
            if 0 <= t < TAPS:
                hit = index == value
                outs = [jnp.where(hit, taps[t], v) for taps, v in zip(sets, outs)]
        return outs

    xs = picked(xi, [(x, x) for x in range(TAPS)])
    for delta in (1, 2):
        ys = picked(yi, [(k, MID + k // delta) for k in range(-7, 8) if k % delta == 0])
        for n, (a, c) in enumerate(TYPES):
            base = xs[a] * ys[c]
            pair = jnp.concatenate([base, pltpu.roll(base, 8, 1)], axis=0)
            slot = (delta - 1) * len(TYPES) + n
            for m in range(BLOCK // 2):
                hi, lo = halves(pair if m == 0 else pltpu.roll(pair, 16 * m, 1))
                dh[slot, pl.ds(m * 16, 16)] = hi
                dl[slot, pl.ds(m * 16, 16)] = lo


def exchange(
    ny, even_in, odd_in, low_in, density, ext, zt1, zt2, wx, cy0, dh, dl,
    even, odd, low, zsend, zrecv, psend, precv, own, tapsem,
):
    rows = density.shape[0]
    nz = density.shape[1]
    halo = HALO * ny
    part = halo // 2
    chunk = part // CHUNKS
    count = lax.axis_size("space")
    space = lax.axis_index("space")
    wave = lax.axis_index("wave")
    core = lax.rem(wave, 2)
    partner = wave + 1 - 2 * core
    above = space < count - 1
    below = space > 0
    barrier = pltpu.get_barrier_semaphore()

    @pl.when(above)
    def _():
        pl.semaphore_signal(barrier, 1, device_id={"space": space + 1}, device_id_type=MESH)

    @pl.when(below)
    def _():
        pl.semaphore_signal(barrier, 1, device_id={"space": space - 1}, device_id_type=MESH)

    pl.semaphore_signal(barrier, 1, device_id={"wave": partner}, device_id_type=MESH)
    fetches = [
        pltpu.make_async_copy(src, dst, tapsem.at[n])
        for n, (src, dst) in enumerate(((even_in, even), (odd_in, odd), (low_in, low)))
    ]
    for fetch in fetches:
        fetch.start()
    inner = pltpu.make_async_copy(density, ext.at[pl.ds(halo, rows)], own)
    inner.start()
    starts = (0, halo + rows)
    arrives = (below, above)
    for way in range(2):

        @pl.when(jnp.logical_not(arrives[way]))
        def _():
            ext[pl.ds(starts[way], halo)] = jnp.zeros((halo, nz), F32)

    peers = 1 + above.astype(jnp.int32) + below.astype(jnp.int32)
    pl.semaphore_wait(barrier, peers)
    sends = (above, below)

    def zcopy(way, q):
        r = core * part + q * chunk
        return pltpu.make_async_remote_copy(
            src_ref=density.at[pl.ds(r + (rows - halo if way == 0 else 0), chunk)],
            dst_ref=ext.at[pl.ds(starts[way] + r, chunk)],
            send_sem=zsend.at[way, q],
            recv_sem=zrecv.at[way, q],
            device_id={"space": space + 1 if way == 0 else space - 1},
            device_id_type=MESH,
        )

    def pcopy(way, q, first):
        piece = ext.at[pl.ds(starts[way] + first * part + q * chunk, chunk)]
        return pltpu.make_async_remote_copy(
            src_ref=piece,
            dst_ref=piece,
            send_sem=psend.at[way, q],
            recv_sem=precv.at[way, q],
            device_id={"wave": partner},
            device_id_type=MESH,
        )

    every = [(way, q) for q in range(CHUNKS) for way in range(2)]
    for way, q in every:

        @pl.when(sends[way])
        def _():
            zcopy(way, q).start()

    for fetch in fetches:
        fetch.wait()
    build_tables(even, odd, low, zt1, zt2, wx, cy0, dh, dl)
    inner.wait()
    for way, q in every:

        @pl.when(arrives[way])
        def _():
            zcopy(way, q).wait_recv()
            pcopy(way, q, core).start()

    for way, q in every:

        @pl.when(sends[way])
        def _():
            zcopy(way, q).wait_send()

        @pl.when(arrives[way])
        def _():
            pcopy(way, q, core).wait_send()
            pcopy(way, q, 1 - core).wait_recv()


def dot(a, b):
    return jnp.dot(a, b, preferred_element_type=F32)


def magnitude(v):
    sq = v * v
    a = sq + pltpu.roll(sq, v.shape[1] // 2, 1) + 1e-06
    return a * lax.rsqrt(a)


def turned(planes, coeffs):
    total = None
    for v, c in zip(planes, coeffs):
        for s in range(8):
            term = c[s] * (v if s == 0 else pltpu.roll(v, s, 0))
            total = term if total is None else total + term
    return total


def kernel(ny, wav_in, pairs_in, ext, zt1, zt2, wx, cy0, dh, dl, out, wav, pairs, hl, zp0, zp1, eb, u, flags, sems):
    nz = ext.shape[1]
    per_dev = out.shape[0]
    outs = out.shape[1]
    spots = outs + REACH2
    pad = REACH2 // 2
    slots = outs + HALO
    space = lax.axis_index("space")
    last = lax.axis_size("space") - 1
    start = lax.axis_index("wave") * per_dev
    fetches = [pltpu.make_async_copy(src, dst, sems.at[n]) for n, (src, dst) in enumerate(((wav_in, wav), (pairs_in, pairs)))]
    for fetch in fetches:
        fetch.start()

    def split_rows(c, carry):
        for ypar in range(2):
            v = ext[pl.ds(c * 4 * ny + ypar, 32, stride=2), :]
            hi, lo = halves(v.reshape(2, 2, 8, nz))
            for xpar in range(2):
                both = jnp.concatenate([hi[:, xpar].reshape(16, nz), lo[:, xpar].reshape(16, nz)], axis=1)
                hl[xpar * 2 + ypar, c] = both
        return carry

    lax.fori_loop(0, slots // 2, split_rows, 0)
    for n in range(2):
        zp1[n, slots // 2] = jnp.zeros((16, 2 * nz), BF)
    for g in range(PAIR_GROUP):
        u[g, pl.ds(spots, 4)] = jnp.zeros((4, 8, nz), F32)

    for fetch in fetches:
        fetch.wait()

    def key_of(f):
        return wav[0, f] * 3 + wav[1, f]

    for k in range(KEYS + 1):
        flags[k] = 0
    for p in range(per_dev):
        f = pairs[0, start + p]
        flags[jnp.where(f < 0, KEYS, key_of(jnp.maximum(f, 0)))] = 1

    def beside(v):
        return jnp.concatenate(halves(v), axis=1)

    def folded(r):
        return r[:, :nz] + r[:, nz:]

    used = slots // 2 - 3
    for n in range(2):
        need = flags[2] if n else flags[0] + flags[1]

        @pl.when(need > 0)
        def _():
            def zpass(q, carry):
                r = folded(dot(hl[q, pl.ds(1, used)].reshape(used * 16, 2 * nz), zt1[n]))
                zp0[n * 4 + q, pl.ds(2, 2 * used)] = r.reshape(2 * used, 8, nz)
                return carry

            lax.fori_loop(0, 4, zpass, 0)

        need = flags[5] if n else flags[3] + flags[4]

        @pl.when(need > 0)
        def _():
            r = folded(dot(hl[0].reshape(slots * 8, 2 * nz), zt1[2 + n]))
            zp1[n, pl.ds(0, slots // 2)] = beside(r).reshape(slots // 2, 16, 2 * nz)

    def store_field(key, at_block, v):
        hi = v.astype(BF)
        lane = lax.broadcasted_iota(jnp.int32, v.shape, 1)
        mixed = jnp.where(lane < nz // 2, v, v - hi.astype(F32)).astype(BF)
        both = jnp.concatenate([mixed, hi], axis=1)
        count = v.shape[0] // 16
        eb[key, pl.ds(at_block, count)] = both.reshape(count, 16, 2 * nz)

    def kinds(o):
        return (o == 0).astype(jnp.int32), (o == 1).astype(jnp.int32), (o == 2).astype(jnp.int32)

    def level0(o, carry):
        @pl.when(flags[o] > 0)
        def _():
            kx, ky, kz = kinds(o)

            def group(c, inner_carry):
                i = c * FIELD_GROUP
                accs = [[None, None] for _ in range(FIELD_GROUP)]
                for t in range(TAPS):
                    w = wx[kx * TAPS + t]
                    xpar = (t + 1) % 2
                    j = (t + MID) // 2
                    for par in range(2):
                        src = kz * 4 + xpar * 2 + par
                        for g in range(FIELD_GROUP):
                            term = w * zp0[src, i + g + j]
                            accs[g][par] = term if t == 0 else accs[g][par] + term
                coeffs = [[cy0[(ky * 2 + par) * 8 + s] for s in range(8)] for par in range(2)]
                v = jnp.concatenate([magnitude(turned(a, coeffs)) for a in accs], axis=0)
                store_field(o, c * (FIELD_GROUP // 2), v)
                return inner_carry

            lax.fori_loop(0, spots // FIELD_GROUP, group, 0)

        return carry

    lax.fori_loop(0, 3, level0, 0)

    def operate(slot, rhs):
        size = BLOCK * 8
        high = dh[pl.ds(slot, 2)].reshape(2 * size, WIDE)
        low = dl[pl.ds(slot, 2)].reshape(2 * size, WIDE)
        ends = dot(low, jnp.concatenate([r[:, :nz] for r in rhs], axis=1))
        lane = lax.broadcasted_iota(jnp.int32, (size, nz), 1)
        result = []
        for b, r in enumerate(rhs):
            v = folded(dot(high, r)) + ends[:, b * nz : (b + 1) * nz]
            result.append(magnitude(jnp.where(lane < nz // 2, v[:size], v[size:])))
        return result

    def level1(o, carry):
        @pl.when(flags[3 + o] > 0)
        def _():
            places = [*range(0, spots - BLOCK, BLOCK), spots - BLOCK]
            for n in range(0, len(places), 2):
                two = places[n : n + 2]
                rhs = [zp1[o // 2, pl.ds(i // 2, 16)].reshape(WIDE, 2 * nz) for i in two]
                for i, v in zip(two, operate(2 * o, rhs)):
                    store_field(3 + o, i // 2, v)

        return carry

    lax.fori_loop(0, 3, level1, 0)

    edge = pad // 2

    @pl.when(space == 0)
    def _():
        for k in range(KEYS):
            eb[k, pl.ds(0, edge)] = jnp.zeros((edge, 16, 2 * nz), BF)

    @pl.when(space == last)
    def _():
        for k in range(KEYS):
            eb[k, pl.ds(spots // 2 - edge, edge)] = jnp.zeros((edge, 16, 2 * nz), BF)

    def second(group, carry):
        p0 = group * PAIR_GROUP
        alive = pairs[0, start + p0] >= 0

        @pl.when(alive)
        def _():
            def ahead(g):
                f = jnp.maximum(pairs[0, start + p0 + g], 0)
                w = pairs[1, start + p0 + g]
                lhs = eb[key_of(f)].reshape(spots * 8, 2 * nz)
                table = (jnp.maximum(wav[0, w], 1) - 1) * 2 + wav[1, w] // 2
                u[g, pl.ds(0, spots)] = dot(lhs, zt2[table]).reshape(spots, 8, nz)

            ahead(0)
            for g in range(PAIR_GROUP):
                if g + 1 < PAIR_GROUP:
                    ahead(g + 1)
                live = pairs[0, start + p0 + g] >= 0
                w = pairs[1, start + p0 + g]
                step = jnp.maximum(wav[0, w], 1)
                begins = [jnp.where(step == 1, b * BLOCK, b) for b in range(2)]
                base = jnp.where(step == 1, pad - MID, 0)
                rhs = [beside(jnp.concatenate([u[g, base + begin + step * m] for m in range(32)], axis=0)) for begin in begins]
                for begin, v in zip(begins, operate((step - 1) * len(TYPES) + 2 * wav[1, w], rhs)):
                    v = jnp.where(live, v, 0.0)
                    for m in range(BLOCK):
                        out[p0 + g, begin + step * m] = v[8 * m : 8 * m + 8, : nz // 2]

        @pl.when(jnp.logical_not(alive))
        def _():
            out[pl.ds(p0, PAIR_GROUP)] = jnp.zeros((PAIR_GROUP,) + out.shape[1:], F32)

        return carry

    lax.fori_loop(0, per_dev // PAIR_GROUP, second, 0)


def shards(density, even_taps, odd_taps, low_taps, wavelets, pairs):
    rows, ny, nz = density.shape
    per_dev = pairs.shape[0] // lax.axis_size("wave")
    flat = density.reshape(rows * ny, nz)
    vmem = pl.BlockSpec(memory_space=pltpu.VMEM)
    hbm = pl.BlockSpec(memory_space=pltpu.HBM)
    shape = jax.ShapeDtypeStruct
    dec = shape((2 * len(TYPES), BLOCK * 8, WIDE), BF)
    tables = (
        shape((4, 2 * nz, 2 * nz), BF),
        shape((4, 2 * nz, nz), BF),
        shape((2 * TAPS, 8, nz), F32),
        shape((32, 8, nz), F32),
        dec,
        dec,
    )
    slots = rows // 2 + HALO
    spots = rows // 2 + REACH2
    prepared = pl.pallas_call(
        functools.partial(exchange, ny),
        out_shape=(shape(((rows + 2 * HALO) * ny, nz), F32), *tables),
        in_specs=[hbm] * 4,
        out_specs=[vmem] * 7,
        scratch_shapes=[pltpu.SMEM((TAPS,), F32)] * 3
        + [pltpu.SemaphoreType.DMA((2, CHUNKS))] * 4
        + [pltpu.SemaphoreType.DMA, pltpu.SemaphoreType.DMA((3,))],
        compiler_params=pltpu.CompilerParams(collective_id=0, has_side_effects=True, vmem_limit_bytes=LIMIT1),
        name="exchange",
    )(*(pltpu.with_memory_space_constraint(v, pltpu.HBM) for v in (even_taps, odd_taps, low_taps, flat)))
    wav, who = (pltpu.with_memory_space_constraint(v.T, pltpu.HBM) for v in (wavelets, pairs))
    return pl.pallas_call(
        functools.partial(kernel, ny),
        out_shape=shape((per_dev, rows // 2, ny // 2, nz // 2), F32),
        in_specs=[hbm] * 2 + [vmem] * 7,
        out_specs=vmem,
        scratch_shapes=[
            pltpu.SMEM(wav.shape, jnp.int32),
            pltpu.SMEM(who.shape, jnp.int32),
            pltpu.VMEM((4, slots // 2, 16, 2 * nz), BF),
            pltpu.VMEM((8, slots, 8, nz), F32),
            pltpu.VMEM((2, slots // 2 + 1, 16, 2 * nz), BF),
            pltpu.VMEM((KEYS, spots // 2, 16, 2 * nz), BF),
            pltpu.VMEM((PAIR_GROUP, spots + 4, 8, nz), F32),
            pltpu.SMEM((KEYS + 1,), jnp.int32),
            pltpu.SemaphoreType.DMA((2,)),
        ],
        compiler_params=pltpu.CompilerParams(vmem_limit_bytes=LIMIT2),
        name="scatter",
    )(wav, who, *prepared)


def solution(mesh):
    placed = (P(("groups", "space"), None, None), P(), P(), P(), P(), P())
    return jax.shard_map(
        shards,
        mesh=mesh,
        in_specs=placed,
        out_specs=P("wave", ("groups", "space"), None, None),
        check_vma=False,
    )
```

```python
import functools

import jax
import jax.numpy as jnp
from jax import lax
from jax.experimental import pallas as pl
from jax.experimental.pallas import tpu as pltpu
from jax.sharding import PartitionSpec as P

REACH1 = 14
REACH2 = 28
HALO = REACH1 + REACH2
TAPS = 15
MID = TAPS // 2
CHUNKS = 3
KEYS = 6
FIELD_GROUP = 6
PAIR_GROUP = 4
BLOCK = 16
WIDE = 256
LIMIT1 = 16 << 20
LIMIT2 = 24 << 20
TYPES = (((0, 2), (1, 2)), ((2, 0), (2, 1)), ((2, 2), (2, 2)))
BF = jnp.bfloat16
F32 = jnp.float32
MESH = pl.DeviceIdType.MESH


def halves(v):
    hi = v.astype(BF)
    return hi, (v - hi.astype(F32)).astype(BF)


def at(taps, t):
    return taps[t] if 0 <= t < TAPS else jnp.float32(0.0)


def build_tables(even, odd, low, zt1, zt2, wx, cy0, dh, dl):
    nz = zt1.shape[1] // 2
    half = nz // 2
    lane8 = lax.broadcasted_iota(jnp.int32, (8, nz), 1)
    sub8 = lax.broadcasted_iota(jnp.int32, (8, nz), 0)

    def split(t):
        return jnp.where(lane8 < half, at(even, t), at(odd, t))

    def plain(t):
        return jnp.full((8, nz), at(low, t), F32)

    for n, kind in enumerate((plain, split)):
        for t in range(TAPS):
            wx[n * TAPS + t] = kind(t)
        for par in range(2):
            for s in range(8):
                k = par - 2 * s
                cy0[(n * 2 + par) * 8 + s] = jnp.where(sub8 >= s, kind(MID + k), kind(MID + 16 + k))

    blk = 32
    row = lax.broadcasted_iota(jnp.int32, (blk, nz), 0)
    col = lax.broadcasted_iota(jnp.int32, (blk, nz), 1)
    wide = jnp.where(col < half, col, col - half)
    is_left = col < half

    def bands(diff, step):
        lo = jnp.zeros((blk, nz), F32)
        eo = jnp.zeros((blk, nz), F32)
        for t in range(TAPS):
            hit = diff == (t - MID) * step
            lo = jnp.where(hit, low[t], lo)
            eo = jnp.where(hit, jnp.where(is_left, even[t], odd[t]), eo)
        return lo, eo

    for level in (0, 1):
        for r0 in range(0, nz, blk):
            for n, v in enumerate(bands(row + r0 - 2 * wide, 1 << level)):
                hi, lo = halves(v)
                ref = zt1.at[level * 2 + n]
                ref[pl.ds(r0, blk), pl.ds(0, nz)] = hi
                ref[pl.ds(r0, blk), pl.ds(nz, nz)] = lo
                ref[pl.ds(nz + r0, blk), pl.ds(0, nz)] = hi
                ref[pl.ds(nz + r0, blk), pl.ds(nz, nz)] = jnp.zeros_like(lo)
    for delta in (1, 2):
        for r0 in range(0, half, blk):
            for n, v in enumerate(bands(row + r0 - wide, delta)):
                hi, lo = halves(v)
                ref = zt2.at[(delta - 1) * 2 + n]
                ref[pl.ds(r0, blk)] = hi
                ref[pl.ds(half + r0, blk)] = hi
                ref[pl.ds(2 * half + r0, blk)] = lo
                ref[pl.ds(3 * half + r0, blk)] = jnp.zeros_like(lo)

    lane = lax.broadcasted_iota(jnp.int32, (8, WIDE), 1)
    xi = lane // 8
    yi = lane % 8 - lax.broadcasted_iota(jnp.int32, (8, WIDE), 0)
    sets = (even, odd, low)

    def picked(index, pairs):
        outs = [jnp.zeros((8, WIDE), F32) for _ in sets]
        for value, t in pairs:
            if 0 <= t < TAPS:
                hit = index == value
                outs = [jnp.where(hit, taps[t], v) for taps, v in zip(sets, outs)]
        return outs

    xs = picked(xi, [(x, x) for x in range(TAPS)])
    for delta in (1, 2):
        ys = picked(yi, [(k, MID + k // delta) for k in range(-7, 8) if k % delta == 0])
        for n, kinds in enumerate(TYPES):
            pair = jnp.concatenate([xs[a] * ys[c] for a, c in kinds], axis=0)
            slot = (delta - 1) * len(TYPES) + n
            for m in range(BLOCK):
                hi, lo = halves(pair if m == 0 else pltpu.roll(pair, 8 * m, 1))
                dh[slot, pl.ds(m * 16, 16)] = hi
                dl[slot, pl.ds(m * 16, 16)] = lo


def dot(a, b):
    return jnp.dot(a, b, preferred_element_type=F32)


def magnitude(v):
    sq = v * v
    a = sq + pltpu.roll(sq, v.shape[1] // 2, 1) + 1e-06
    return a * lax.rsqrt(a)


def turned(planes, coeffs):
    total = None
    for v, c in zip(planes, coeffs):
        for s in range(8):
            term = c[s] * (v if s == 0 else pltpu.roll(v, s, 0))
            total = term if total is None else total + term
    return total


def beside(v):
    return jnp.concatenate(halves(v), axis=1)


def folded(r):
    n = r.shape[1] // 2
    return r[:, :n] + r[:, n:]


def paired(v):
    hi = v.astype(BF)
    lane = lax.broadcasted_iota(jnp.int32, v.shape, 1)
    mixed = jnp.where(lane < v.shape[1] // 2, v, v - hi.astype(F32)).astype(BF)
    return jnp.concatenate([mixed, hi], axis=1).reshape(v.shape[0] // 16, 16, 2 * v.shape[1])


def divided(ext, at_row, ny):
    nz = ext.shape[1]
    out = [None] * 4
    for ypar in range(2):
        v = ext[pl.ds(at_row * ny + ypar, 32, stride=2), :]
        hi, lo = halves(v.reshape(2, 2, 8, nz))
        for xpar in range(2):
            out[xpar * 2 + ypar] = jnp.concatenate([hi[:, xpar].reshape(16, nz), lo[:, xpar].reshape(16, nz)], axis=1)
    return out


def fine_fields(z, wx, cy0, kx, ky, kz, i):
    accs = [[None, None] for _ in range(FIELD_GROUP)]
    for t in range(TAPS):
        w = wx[kx * TAPS + t]
        xpar = (t + 1) % 2
        j = (t + MID) // 2
        for par in range(2):
            src = kz * 4 + xpar * 2 + par
            for g in range(FIELD_GROUP):
                term = w * z[src, i + g + j]
                accs[g][par] = term if t == 0 else accs[g][par] + term
    coeffs = [[cy0[(ky * 2 + par) * 8 + s] for s in range(8)] for par in range(2)]
    return paired(jnp.concatenate([magnitude(turned(a, coeffs)) for a in accs], axis=0))


def exchange(
    ny, even_in, odd_in, low_in, density, ext, zt1, zt2, wx, cy0, dh, dl, early,
    even, odd, low, hl, zp, zsend, zrecv, psend, precv, own, tapsem,
):
    rows = density.shape[0]
    nz = density.shape[1]
    halo = HALO * ny
    part = halo // 2
    chunk = part // CHUNKS
    count = lax.axis_size("space")
    space = lax.axis_index("space")
    wave = lax.axis_index("wave")
    core = lax.rem(wave, 2)
    partner = wave + 1 - 2 * core
    above = space < count - 1
    below = space > 0
    barrier = pltpu.get_barrier_semaphore()

    @pl.when(above)
    def _():
        pl.semaphore_signal(barrier, 1, device_id={"space": space + 1}, device_id_type=MESH)

    @pl.when(below)
    def _():
        pl.semaphore_signal(barrier, 1, device_id={"space": space - 1}, device_id_type=MESH)

    pl.semaphore_signal(barrier, 1, device_id={"wave": partner}, device_id_type=MESH)
    fetches = [
        pltpu.make_async_copy(src, dst, tapsem.at[n])
        for n, (src, dst) in enumerate(((even_in, even), (odd_in, odd), (low_in, low)))
    ]
    for fetch in fetches:
        fetch.start()
    inner = pltpu.make_async_copy(density, ext.at[pl.ds(halo, rows)], own)
    inner.start()
    starts = (0, halo + rows)
    arrives = (below, above)
    for way in range(2):

        @pl.when(jnp.logical_not(arrives[way]))
        def _():
            ext[pl.ds(starts[way], halo)] = jnp.zeros((halo, nz), F32)

    peers = 1 + above.astype(jnp.int32) + below.astype(jnp.int32)
    pl.semaphore_wait(barrier, peers)
    sends = (above, below)

    def zcopy(way, q):
        r = core * part + q * chunk
        return pltpu.make_async_remote_copy(
            src_ref=density.at[pl.ds(r + (rows - halo if way == 0 else 0), chunk)],
            dst_ref=ext.at[pl.ds(starts[way] + r, chunk)],
            send_sem=zsend.at[way, q],
            recv_sem=zrecv.at[way, q],
            device_id={"space": space + 1 if way == 0 else space - 1},
            device_id_type=MESH,
        )

    def pcopy(way, q, first):
        piece = ext.at[pl.ds(starts[way] + first * part + q * chunk, chunk)]
        return pltpu.make_async_remote_copy(
            src_ref=piece,
            dst_ref=piece,
            send_sem=psend.at[way, q],
            recv_sem=precv.at[way, q],
            device_id={"wave": partner},
            device_id_type=MESH,
        )

    every = [(way, q) for q in range(CHUNKS) for way in range(2)]
    for way, q in every:

        @pl.when(sends[way])
        def _():
            zcopy(way, q).start()

    for fetch in fetches:
        fetch.wait()
    build_tables(even, odd, low, zt1, zt2, wx, cy0, dh, dl)
    inner.wait()
    blocks = rows // ny // 4

    def split_rows(c, carry):
        for q, both in enumerate(divided(ext, HALO + c * 4, ny)):
            hl[q, c] = both
        return carry

    lax.fori_loop(0, blocks, split_rows, 0)

    def zpass(q, carry):
        v = hl[q].reshape(blocks * 16, 2 * nz)
        tables = [zt1[n] for n in range(2)]
        his, los = (jnp.concatenate([t[:nz, m * nz : (m + 1) * nz] for t in tables], axis=1) for m in range(2))
        r = dot(jnp.concatenate([v, v[:, :nz]], axis=1), jnp.concatenate([his, his, los], axis=0))
        for n in range(2):
            zp[n * 4 + q] = r[:, n * nz : (n + 1) * nz].reshape(2 * blocks, 8, nz)
        return carry

    lax.fori_loop(0, 4, zpass, 0)
    skip = HALO // 2
    begin = (HALO - MID + 1) // 2
    count_early = early.shape[1] * 2 // FIELD_GROUP
    for o in range(3):

        def group(c, carry):
            v = fine_fields(zp, wx, cy0, int(o == 0), int(o == 1), int(o == 2), begin - skip + c * FIELD_GROUP)
            early[o, pl.ds(c * (FIELD_GROUP // 2), FIELD_GROUP // 2)] = v
            return carry

        lax.fori_loop(0, count_early, group, 0)
        for way in range(2):

            @pl.when(arrives[way])
            def _():
                zcopy(way, o).wait_recv()
                pcopy(way, o, core).start()

    for way, q in every:

        @pl.when(sends[way])
        def _():
            zcopy(way, q).wait_send()

        @pl.when(arrives[way])
        def _():
            pcopy(way, q, core).wait_send()
            pcopy(way, q, 1 - core).wait_recv()


def kernel(ny, wav_in, pairs_in, ext, zt1, zt2, wx, cy0, dh, dl, inner, out, wav, pairs, hl, zp0, zp1, eb, flags, sems, *u):
    nz = ext.shape[1]
    per_dev = out.shape[0]
    outs = out.shape[1]
    spots = outs + REACH2
    pad = REACH2 // 2
    slots = outs + HALO
    space = lax.axis_index("space")
    last = lax.axis_size("space") - 1
    start = lax.axis_index("wave") * per_dev
    fetches = [pltpu.make_async_copy(src, dst, sems.at[n]) for n, (src, dst) in enumerate(((wav_in, wav), (pairs_in, pairs)))]
    for fetch in fetches:
        fetch.start()

    def split_rows(c, carry):
        for q, both in enumerate(divided(ext, c * 4, ny)):
            hl[q, c] = both
        return carry

    lax.fori_loop(0, slots // 2, split_rows, 0)
    for n in range(2):
        zp1[n, slots // 2] = jnp.zeros((16, 2 * nz), BF)
    for g in range(PAIR_GROUP):
        u[g][pl.ds(spots, 4)] = jnp.zeros((4, 8, nz), F32)

    for fetch in fetches:
        fetch.wait()

    def key_of(f):
        return wav[0, f] * 3 + wav[1, f]

    for k in range(KEYS + 1):
        flags[k] = 0
    for p in range(per_dev):
        f = pairs[0, start + p]
        flags[jnp.where(f < 0, KEYS, key_of(jnp.maximum(f, 0)))] = 1

    groups = spots // FIELD_GROUP
    early = inner.shape[1] * 2 // FIELD_GROUP
    begin = (groups - early) // 2
    side = begin * FIELD_GROUP // 2 + 4
    other = slots // 2 - 2 - side
    for n in range(2):
        need = flags[2] if n else flags[0] + flags[1]

        @pl.when(need > 0)
        def _():
            def zpass(k, carry):
                q = k // 2
                at_block = 1 + (k % 2) * (other - 1)
                r = folded(dot(hl[q, pl.ds(at_block, side)].reshape(side * 16, 2 * nz), zt1[n]))
                zp0[n * 4 + q, pl.ds(2 * at_block, 2 * side)] = r.reshape(2 * side, 8, nz)
                return carry

            lax.fori_loop(0, 8, zpass, 0)

        need = flags[5] if n else flags[3] + flags[4]

        @pl.when(need > 0)
        def _():
            r = folded(dot(hl[0].reshape(slots * 8, 2 * nz), zt1[2 + n]))
            zp1[n, pl.ds(0, slots // 2)] = beside(r).reshape(slots // 2, 16, 2 * nz)

    def kinds(o):
        return (o == 0).astype(jnp.int32), (o == 1).astype(jnp.int32), (o == 2).astype(jnp.int32)

    def level0(o, carry):
        @pl.when(flags[o] > 0)
        def _():
            kx, ky, kz = kinds(o)

            eb[o, pl.ds(begin * FIELD_GROUP // 2, inner.shape[1])] = inner[o]

            def group(k, inner_carry):
                c = jnp.where(k < begin, k, k + early)
                v = fine_fields(zp0, wx, cy0, kx, ky, kz, c * FIELD_GROUP)
                eb[o, pl.ds(c * (FIELD_GROUP // 2), FIELD_GROUP // 2)] = v
                return inner_carry

            lax.fori_loop(0, groups - early, group, 0)

        return carry

    lax.fori_loop(0, 3, level0, 0)

    def operate(slot, rhs):
        high, low = dh[slot], dl[slot]
        his, los = (jnp.concatenate([r[n] for r in rhs], axis=1) for n in range(2))
        r = dot(jnp.concatenate([high, high, low], axis=1), jnp.concatenate([his, los, his], axis=0))
        lane = lax.broadcasted_iota(jnp.int32, (BLOCK, 8, nz), 2)
        result = []
        for b in range(2):
            v = r[:, b * nz : (b + 1) * nz].reshape(BLOCK, 2, 8, nz)
            result.append(magnitude(jnp.where(lane < nz // 2, v[:, 0], v[:, 1]).reshape(BLOCK * 8, nz)))
        return result

    def level1(o, carry):
        @pl.when(flags[3 + o] > 0)
        def _():
            places = [*range(0, spots - BLOCK, BLOCK), spots - BLOCK]
            for n in range(0, len(places), 2):
                two = places[n : n + 2]
                both = [zp1[o // 2, pl.ds(i // 2, 16)].reshape(WIDE, 2 * nz) for i in two]
                rhs = [(r[:, :nz], r[:, nz:]) for r in both]
                for i, v in zip(two, operate(o, rhs)):
                    eb[3 + o, pl.ds(i // 2, BLOCK // 2)] = paired(v)

        return carry

    lax.fori_loop(0, 3, level1, 0)

    edge = pad // 2

    @pl.when(space == 0)
    def _():
        for k in range(KEYS):
            eb[k, pl.ds(0, edge)] = jnp.zeros((edge, 16, 2 * nz), BF)

    @pl.when(space == last)
    def _():
        for k in range(KEYS):
            eb[k, pl.ds(spots // 2 - edge, edge)] = jnp.zeros((edge, 16, 2 * nz), BF)

    def second(group, carry):
        p0 = group * PAIR_GROUP
        alive = pairs[0, start + p0] >= 0

        @pl.when(alive)
        def _():
            def ahead(g):
                f = jnp.maximum(pairs[0, start + p0 + g], 0)
                w = pairs[1, start + p0 + g]
                lhs = eb[key_of(f)].reshape(spots * 8, 2 * nz)
                table = (jnp.maximum(wav[0, w], 1) - 1) * 2 + wav[1, w] // 2
                u[g][pl.ds(0, spots)] = dot(lhs, zt2[table]).reshape(spots, 8, nz)

            ahead(0)
            for g in range(PAIR_GROUP):
                if g + 1 < PAIR_GROUP:
                    ahead(g + 1)
                live = pairs[0, start + p0 + g] >= 0
                w = pairs[1, start + p0 + g]
                step = jnp.maximum(wav[0, w], 1)
                begins = [jnp.where(step == 1, b * BLOCK, b) for b in range(2)]
                base = jnp.where(step == 1, pad - MID, 0)
                rhs = [halves(jnp.concatenate([u[g][base + begin + step * m] for m in range(32)], axis=0)) for begin in begins]
                for begin, v in zip(begins, operate((step - 1) * len(TYPES) + wav[1, w], rhs)):
                    v = jnp.where(live, v, 0.0)
                    for m in range(BLOCK):
                        out[p0 + g, begin + step * m] = v[8 * m : 8 * m + 8, : nz // 2]

        @pl.when(jnp.logical_not(alive))
        def _():
            out[pl.ds(p0, PAIR_GROUP)] = jnp.zeros((PAIR_GROUP,) + out.shape[1:], F32)

        return carry

    lax.fori_loop(0, per_dev // PAIR_GROUP, second, 0)


def shards(density, even_taps, odd_taps, low_taps, wavelets, pairs):
    rows, ny, nz = density.shape
    per_dev = pairs.shape[0] // lax.axis_size("wave")
    flat = density.reshape(rows * ny, nz)
    vmem = pl.BlockSpec(memory_space=pltpu.VMEM)
    hbm = pl.BlockSpec(memory_space=pltpu.HBM)
    shape = jax.ShapeDtypeStruct
    dec = shape((2 * len(TYPES), BLOCK * 16, WIDE), BF)
    tables = (
        shape((4, 2 * nz, 2 * nz), BF),
        shape((4, 2 * nz, nz), BF),
        shape((2 * TAPS, 8, nz), F32),
        shape((32, 8, nz), F32),
        dec,
        dec,
    )
    slots = rows // 2 + HALO
    spots = rows // 2 + REACH2
    blocks = rows // 4
    early = (rows - 2 * MID - 2) // 2 // FIELD_GROUP * FIELD_GROUP
    prepared = pl.pallas_call(
        functools.partial(exchange, ny),
        out_shape=(shape(((rows + 2 * HALO) * ny, nz), F32), *tables, shape((3, early // 2, 16, 2 * nz), BF)),
        in_specs=[hbm] * 4,
        out_specs=[vmem] * 8,
        scratch_shapes=[pltpu.SMEM((TAPS,), F32)] * 3
        + [pltpu.VMEM((4, blocks, 16, 2 * nz), BF), pltpu.VMEM((8, 2 * blocks, 8, nz), F32)]
        + [pltpu.SemaphoreType.DMA((2, CHUNKS))] * 4
        + [pltpu.SemaphoreType.DMA, pltpu.SemaphoreType.DMA((3,))],
        compiler_params=pltpu.CompilerParams(collective_id=0, has_side_effects=True, vmem_limit_bytes=LIMIT1),
        name="exchange",
    )(*(pltpu.with_memory_space_constraint(v, pltpu.HBM) for v in (even_taps, odd_taps, low_taps, flat)))
    wav, who = (pltpu.with_memory_space_constraint(v.T, pltpu.HBM) for v in (wavelets, pairs))
    return pl.pallas_call(
        functools.partial(kernel, ny),
        out_shape=shape((per_dev, rows // 2, ny // 2, nz // 2), F32),
        in_specs=[hbm] * 2 + [vmem] * 8,
        out_specs=vmem,
        scratch_shapes=[
            pltpu.SMEM(wav.shape, jnp.int32),
            pltpu.SMEM(who.shape, jnp.int32),
            pltpu.VMEM((4, slots // 2, 16, 2 * nz), BF),
            pltpu.VMEM((8, slots, 8, nz), F32),
            pltpu.VMEM((2, slots // 2 + 1, 16, 2 * nz), BF),
            pltpu.VMEM((KEYS, spots // 2, 16, 2 * nz), BF),
            pltpu.SMEM((KEYS + 1,), jnp.int32),
            pltpu.SemaphoreType.DMA((2,)),
        ]
        + [pltpu.VMEM((spots + 4, 8, nz), F32)] * PAIR_GROUP,
        compiler_params=pltpu.CompilerParams(vmem_limit_bytes=LIMIT2),
        name="scatter",
    )(wav, who, *prepared)


def solution(mesh):
    placed = (P(("groups", "space"), None, None), P(), P(), P(), P(), P())
    return jax.shard_map(
        shards,
        mesh=mesh,
        in_specs=placed,
        out_specs=P("wave", ("groups", "space"), None, None),
        check_vma=False,
    )
```

```python
import functools

import jax
import jax.numpy as jnp
from jax import lax
from jax.experimental import pallas as pl
from jax.experimental.pallas import tpu as pltpu
from jax.sharding import PartitionSpec as P

REACH1 = 14
REACH2 = 28
HALO = REACH1 + REACH2
TAPS = 15
MID = TAPS // 2
CHUNKS = 3
KEYS = 6
FIELD_GROUP = 6
PAIR_GROUP = 8
BLOCK = 16
WIDE = 256
LIMIT1 = 16 << 20
LIMIT2 = 24 << 20
TYPES = (((0, 2), (1, 2)), ((2, 0), (2, 1)), ((2, 2), (2, 2)))
BF = jnp.bfloat16
F32 = jnp.float32
MESH = pl.DeviceIdType.MESH


def halves(v):
    hi = v.astype(BF)
    return hi, (v - hi.astype(F32)).astype(BF)


def at(taps, t):
    return taps[t] if 0 <= t < TAPS else jnp.float32(0.0)


def build_tables(even, odd, low, zt1, zt2, wx, cy0, dh, dl):
    nz = zt1.shape[1] // 2
    half = nz // 2
    lane8 = lax.broadcasted_iota(jnp.int32, (8, nz), 1)
    sub8 = lax.broadcasted_iota(jnp.int32, (8, nz), 0)

    def split(t):
        return jnp.where(lane8 < half, at(even, t), at(odd, t))

    def plain(t):
        return jnp.full((8, nz), at(low, t), F32)

    for n, kind in enumerate((plain, split)):
        for t in range(TAPS):
            wx[n * TAPS + t] = kind(t)
        for par in range(2):
            for s in range(8):
                k = par - 2 * s
                cy0[(n * 2 + par) * 8 + s] = jnp.where(sub8 >= s, kind(MID + k), kind(MID + 16 + k))

    blk = 32
    row = lax.broadcasted_iota(jnp.int32, (blk, nz), 0)
    col = lax.broadcasted_iota(jnp.int32, (blk, nz), 1)
    wide = jnp.where(col < half, col, col - half)
    is_left = col < half

    def bands(diff, step):
        lo = jnp.zeros((blk, nz), F32)
        eo = jnp.zeros((blk, nz), F32)
        for t in range(TAPS):
            hit = diff == (t - MID) * step
            lo = jnp.where(hit, low[t], lo)
            eo = jnp.where(hit, jnp.where(is_left, even[t], odd[t]), eo)
        return lo, eo

    for level in (0, 1):
        for r0 in range(0, nz, blk):
            for n, v in enumerate(bands(row + r0 - 2 * wide, 1 << level)):
                hi, lo = halves(v)
                ref = zt1.at[level * 2 + n]
                ref[pl.ds(r0, blk), pl.ds(0, nz)] = hi
                ref[pl.ds(r0, blk), pl.ds(nz, nz)] = lo
                ref[pl.ds(nz + r0, blk), pl.ds(0, nz)] = hi
                ref[pl.ds(nz + r0, blk), pl.ds(nz, nz)] = jnp.zeros_like(lo)
    for delta in (1, 2):
        for r0 in range(0, half, blk):
            for n, v in enumerate(bands(row + r0 - wide, delta)):
                hi, lo = halves(v)
                ref = zt2.at[(delta - 1) * 2 + n]
                ref[pl.ds(r0, blk)] = hi
                ref[pl.ds(half + r0, blk)] = hi
                ref[pl.ds(2 * half + r0, blk)] = lo
                ref[pl.ds(3 * half + r0, blk)] = jnp.zeros_like(lo)

    lane = lax.broadcasted_iota(jnp.int32, (8, WIDE), 1)
    xi = lane // 8
    yi = lane % 8 - lax.broadcasted_iota(jnp.int32, (8, WIDE), 0)
    sets = (even, odd, low)

    def picked(index, pairs):
        outs = [jnp.zeros((8, WIDE), F32) for _ in sets]
        for value, t in pairs:
            if 0 <= t < TAPS:
                hit = index == value
                outs = [jnp.where(hit, taps[t], v) for taps, v in zip(sets, outs)]
        return outs

    xs = picked(xi, [(x, x - 1) for x in range(1, TAPS + 1)])
    for delta in (1, 2):
        ys = picked(yi, [(k, MID + k // delta) for k in range(-7, 8) if k % delta == 0])
        for n, kinds in enumerate(TYPES):
            pair = jnp.concatenate([xs[a] * ys[c] for a, c in kinds], axis=0)
            slot = (delta - 1) * len(TYPES) + n
            for m in range(BLOCK):
                hi, lo = halves(pair if m == 0 else pltpu.roll(pair, 8 * m, 1))
                dh[slot, pl.ds(m * 16, 16)] = hi
                dl[slot, pl.ds(m * 16, 16)] = lo


def dot(a, b):
    return jnp.dot(a, b, preferred_element_type=F32)


def magnitude(v):
    sq = v * v
    a = sq + pltpu.roll(sq, v.shape[1] // 2, 1) + 1e-06
    return a * lax.rsqrt(a)


def turned(planes, coeffs):
    total = None
    for v, c in zip(planes, coeffs):
        for s in range(8):
            term = c[s] * (v if s == 0 else pltpu.roll(v, s, 0))
            total = term if total is None else total + term
    return total


def beside(v):
    return jnp.concatenate(halves(v), axis=1)


def folded(r):
    n = r.shape[1] // 2
    return r[:, :n] + r[:, n:]


def arrange(rows, tiles, spots):
    def parts(x):
        if not 0 <= x < spots:
            return jnp.zeros(rows.shape[1:], F32), jnp.zeros(rows.shape[1:], F32)
        v = rows[x]
        hi = v.astype(BF).astype(F32)
        lane = lax.broadcasted_iota(jnp.int32, v.shape, 1)
        return jnp.where(lane < v.shape[1] // 2, v, v - hi), hi

    def tile(a, b):
        return jnp.concatenate([jnp.concatenate([m, n], axis=0) for m, n in zip(a, b)], axis=1).astype(BF)

    for k in range(spots // 4 + 1):
        got = [parts(4 * k - 2 + n) for n in range(4)]
        for n in range(2):
            if 0 <= 4 * k - 2 + 2 * n < spots:
                tiles[2 * k - 1 + n] = tile(got[2 * n], got[2 * n + 1])
            tiles[spots // 2 + n * BLOCK + k] = tile(got[n], got[n + 2])


def divided(ext, at_row, ny):
    nz = ext.shape[1]
    out = [None] * 4
    for ypar in range(2):
        v = ext[pl.ds(at_row * ny + ypar, 32, stride=2), :]
        hi, lo = halves(v.reshape(2, 2, 8, nz))
        for xpar in range(2):
            out[xpar * 2 + ypar] = jnp.concatenate([hi[:, xpar].reshape(16, nz), lo[:, xpar].reshape(16, nz)], axis=1)
    return out


def fine_fields(z, wx, cy0, kx, ky, kz, i):
    accs = [[None, None] for _ in range(FIELD_GROUP)]
    for t in range(TAPS):
        w = wx[kx * TAPS + t]
        xpar = (t + 1) % 2
        j = (t + MID) // 2
        for par in range(2):
            src = kz * 4 + xpar * 2 + par
            for g in range(FIELD_GROUP):
                term = w * z[src, i + g + j]
                accs[g][par] = term if t == 0 else accs[g][par] + term
    coeffs = [[cy0[(ky * 2 + par) * 8 + s] for s in range(8)] for par in range(2)]
    return [magnitude(turned(a, coeffs)) for a in accs]


def exchange(
    ny, even_in, odd_in, low_in, density, ext, zt1, zt2, wx, cy0, dh, dl, early,
    even, odd, low, hl, zp, zsend, zrecv, psend, precv, own, tapsem,
):
    rows = density.shape[0]
    nz = density.shape[1]
    halo = HALO * ny
    part = halo // 2
    chunk = part // CHUNKS
    count = lax.axis_size("space")
    space = lax.axis_index("space")
    wave = lax.axis_index("wave")
    core = lax.rem(wave, 2)
    partner = wave + 1 - 2 * core
    above = space < count - 1
    below = space > 0
    barrier = pltpu.get_barrier_semaphore()

    @pl.when(above)
    def _():
        pl.semaphore_signal(barrier, 1, device_id={"space": space + 1}, device_id_type=MESH)

    @pl.when(below)
    def _():
        pl.semaphore_signal(barrier, 1, device_id={"space": space - 1}, device_id_type=MESH)

    pl.semaphore_signal(barrier, 1, device_id={"wave": partner}, device_id_type=MESH)
    fetches = [
        pltpu.make_async_copy(src, dst, tapsem.at[n])
        for n, (src, dst) in enumerate(((even_in, even), (odd_in, odd), (low_in, low)))
    ]
    for fetch in fetches:
        fetch.start()
    inner = pltpu.make_async_copy(density, ext.at[pl.ds(halo, rows)], own)
    inner.start()
    starts = (0, halo + rows)
    arrives = (below, above)
    for way in range(2):

        @pl.when(jnp.logical_not(arrives[way]))
        def _():
            ext[pl.ds(starts[way], halo)] = jnp.zeros((halo, nz), F32)

    peers = 1 + above.astype(jnp.int32) + below.astype(jnp.int32)
    pl.semaphore_wait(barrier, peers)
    sends = (above, below)

    def zcopy(way, q):
        r = core * part + q * chunk
        return pltpu.make_async_remote_copy(
            src_ref=density.at[pl.ds(r + (rows - halo if way == 0 else 0), chunk)],
            dst_ref=ext.at[pl.ds(starts[way] + r, chunk)],
            send_sem=zsend.at[way, q],
            recv_sem=zrecv.at[way, q],
            device_id={"space": space + 1 if way == 0 else space - 1},
            device_id_type=MESH,
        )

    def pcopy(way, q, first):
        piece = ext.at[pl.ds(starts[way] + first * part + q * chunk, chunk)]
        return pltpu.make_async_remote_copy(
            src_ref=piece,
            dst_ref=piece,
            send_sem=psend.at[way, q],
            recv_sem=precv.at[way, q],
            device_id={"wave": partner},
            device_id_type=MESH,
        )

    every = [(way, q) for q in range(CHUNKS) for way in range(2)]
    for way, q in every:

        @pl.when(sends[way])
        def _():
            zcopy(way, q).start()

    for fetch in fetches:
        fetch.wait()
    build_tables(even, odd, low, zt1, zt2, wx, cy0, dh, dl)
    inner.wait()
    blocks = rows // ny // 4

    def split_rows(c, carry):
        for q, both in enumerate(divided(ext, HALO + c * 4, ny)):
            hl[q, c] = both
        return carry

    lax.fori_loop(0, blocks, split_rows, 0)

    def zpass(q, carry):
        v = hl[q].reshape(blocks * 16, 2 * nz)
        tables = [zt1[n] for n in range(2)]
        his, los = (jnp.concatenate([t[:nz, m * nz : (m + 1) * nz] for t in tables], axis=1) for m in range(2))
        r = dot(jnp.concatenate([v, v[:, :nz]], axis=1), jnp.concatenate([his, his, los], axis=0))
        for n in range(2):
            zp[n * 4 + q] = r[:, n * nz : (n + 1) * nz].reshape(2 * blocks, 8, nz)
        return carry

    lax.fori_loop(0, 4, zpass, 0)
    skip = HALO // 2
    begin = (HALO - MID + 1) // 2
    count_early = early.shape[1] // FIELD_GROUP
    for o in range(3):

        def group(c, carry):
            v = fine_fields(zp, wx, cy0, int(o == 0), int(o == 1), int(o == 2), begin - skip + c * FIELD_GROUP)
            for g in range(FIELD_GROUP):
                early[o, c * FIELD_GROUP + g] = v[g]
            return carry

        lax.fori_loop(0, count_early, group, 0)
        for way in range(2):

            @pl.when(arrives[way])
            def _():
                zcopy(way, o).wait_recv()
                pcopy(way, o, core).start()

    for way, q in every:

        @pl.when(sends[way])
        def _():
            zcopy(way, q).wait_send()

        @pl.when(arrives[way])
        def _():
            pcopy(way, q, core).wait_send()
            pcopy(way, q, 1 - core).wait_recv()


def kernel(ny, wav_in, pairs_in, ext, zt1, zt2, wx, cy0, dh, dl, inner, out, wav, pairs, hl, zp0, zp1, ef, eb, flags, sems, *stage):
    nz = ext.shape[1]
    per_dev = out.shape[0]
    outs = out.shape[1]
    spots = outs + REACH2
    pad = REACH2 // 2
    slots = outs + HALO
    space = lax.axis_index("space")
    last = lax.axis_size("space") - 1
    start = lax.axis_index("wave") * per_dev
    fetches = [pltpu.make_async_copy(src, dst, sems.at[n]) for n, (src, dst) in enumerate(((wav_in, wav), (pairs_in, pairs)))]
    for fetch in fetches:
        fetch.start()

    def split_rows(c, carry):
        for q, both in enumerate(divided(ext, c * 4, ny)):
            hl[q, c] = both
        return carry

    lax.fori_loop(0, slots // 2, split_rows, 0)

    for fetch in fetches:
        fetch.wait()

    def key_of(f):
        return wav[0, f] * 3 + wav[1, f]

    for k in range(KEYS + 1):
        flags[k] = 0
    for p in range(per_dev):
        f = pairs[0, start + p]
        flags[jnp.where(f < 0, KEYS, key_of(jnp.maximum(f, 0)))] = 1

    groups = spots // FIELD_GROUP
    early = inner.shape[1] // FIELD_GROUP
    begin = (groups - early) // 2
    side = begin * FIELD_GROUP // 2 + 4
    other = slots // 2 - 2 - side
    for n in range(2):
        need = flags[2] if n else flags[0] + flags[1]

        @pl.when(need > 0)
        def _():
            def zpass(k, carry):
                q = k // 2
                at_block = 1 + (k % 2) * (other - 1)
                r = folded(dot(hl[q, pl.ds(at_block, side)].reshape(side * 16, 2 * nz), zt1[n]))
                zp0[n * 4 + q, pl.ds(2 * at_block, 2 * side)] = r.reshape(2 * side, 8, nz)
                return carry

            lax.fori_loop(0, 8, zpass, 0)

        need = flags[5] if n else flags[3] + flags[4]

        @pl.when(need > 0)
        def _():
            r = folded(dot(hl[0].reshape(slots * 8, 2 * nz), zt1[2 + n]))
            none = jnp.zeros((8, nz), F32)
            r = jnp.concatenate([none, r, none], axis=0)
            zp1[n] = beside(r).reshape(slots // 2 + 1, 16, 2 * nz)

    def kinds(o):
        return (o == 0).astype(jnp.int32), (o == 1).astype(jnp.int32), (o == 2).astype(jnp.int32)

    def level0(o, carry):
        @pl.when(flags[o] > 0)
        def _():
            kx, ky, kz = kinds(o)

            ef[o, pl.ds(begin * FIELD_GROUP, inner.shape[1])] = inner[o]

            def group(k, inner_carry):
                c = jnp.where(k < begin, k, k + early)
                v = fine_fields(zp0, wx, cy0, kx, ky, kz, c * FIELD_GROUP)
                for g in range(FIELD_GROUP):
                    ef[o, c * FIELD_GROUP + g] = v[g]
                return inner_carry

            lax.fori_loop(0, groups - early, group, 0)

        return carry

    lax.fori_loop(0, 3, level0, 0)

    def operate(slot, his, los):
        high, low = dh[slot], dl[slot]
        r = dot(jnp.concatenate([high, high, low], axis=1), jnp.concatenate([his, los, his], axis=0))
        lane = lax.broadcasted_iota(jnp.int32, (BLOCK, 8, nz), 2)
        result = []
        for b in range(2):
            v = r[:, b * nz : (b + 1) * nz].reshape(BLOCK, 2, 8, nz)
            result.append(magnitude(jnp.where(lane < nz // 2, v[:, 0], v[:, 1]).reshape(BLOCK * 8, nz)))
        return result

    def level1(o, carry):
        @pl.when(flags[3 + o] > 0)
        def _():
            places = [*range(0, spots - BLOCK, BLOCK), spots - BLOCK]
            for n in range(0, len(places), 2):
                two = places[n : n + 2]
                both = [zp1[o // 2, pl.ds(i // 2, 16)].reshape(WIDE, 2 * nz) for i in two]
                his, los = (jnp.concatenate([r[:, m * nz : (m + 1) * nz] for r in both], axis=1) for m in range(2))
                for i, v in zip(two, operate(o, his, los)):
                    ef[3 + o, pl.ds(i, BLOCK)] = v.reshape(BLOCK, 8, nz)

        return carry

    lax.fori_loop(0, 3, level1, 0)

    @pl.when(space == 0)
    def _():
        for k in range(KEYS):
            ef[k, pl.ds(0, pad)] = jnp.zeros((pad, 8, nz), F32)

    @pl.when(space == last)
    def _():
        for k in range(KEYS):
            ef[k, pl.ds(spots - pad, pad)] = jnp.zeros((pad, 8, nz), F32)

    def spread(k, carry):
        @pl.when(flags[k] > 0)
        def _():
            arrange(ef.at[k], eb.at[k], spots)

        return carry

    lax.fori_loop(0, KEYS, spread, 0)

    def second(group, carry):
        p0 = group * PAIR_GROUP
        alive = pairs[0, start + p0] >= 0

        @pl.when(alive)
        def _():
            def ahead(g):
                key = key_of(jnp.maximum(pairs[0, start + p0 + g], 0))
                w = pairs[1, start + p0 + g]
                step = jnp.maximum(wav[0, w], 1)
                table = zt2[(step - 1) * 2 + wav[1, w] // 2]
                for b in range(2):
                    at_tile = jnp.where(step == 1, (pad - MID - 1) // 2 + b * (BLOCK // 2), spots // 2 + b * BLOCK)
                    hi, lo = halves(dot(eb[key, pl.ds(at_tile, BLOCK)].reshape(WIDE, 2 * nz), table))
                    stage[g][0, :, pl.ds(b * nz, nz)] = hi
                    stage[g][1, :, pl.ds(b * nz, nz)] = lo

            ahead(0)
            for g in range(PAIR_GROUP):
                if g + 1 < PAIR_GROUP:
                    ahead(g + 1)
                live = pairs[0, start + p0 + g] >= 0
                w = pairs[1, start + p0 + g]
                step = jnp.maximum(wav[0, w], 1)
                parts = operate((step - 1) * len(TYPES) + wav[1, w], stage[g][0], stage[g][1])
                for b, v in enumerate(parts):
                    v = jnp.where(live, v, 0.0)
                    begin = jnp.where(step == 1, b * BLOCK, b)
                    for m in range(BLOCK):
                        out[p0 + g, begin + step * m] = v[8 * m : 8 * m + 8, : nz // 2]

        @pl.when(jnp.logical_not(alive))
        def _():
            out[pl.ds(p0, PAIR_GROUP)] = jnp.zeros((PAIR_GROUP,) + out.shape[1:], F32)

        return carry

    lax.fori_loop(0, per_dev // PAIR_GROUP, second, 0)


def shards(density, even_taps, odd_taps, low_taps, wavelets, pairs):
    rows, ny, nz = density.shape
    per_dev = pairs.shape[0] // lax.axis_size("wave")
    flat = density.reshape(rows * ny, nz)
    vmem = pl.BlockSpec(memory_space=pltpu.VMEM)
    hbm = pl.BlockSpec(memory_space=pltpu.HBM)
    shape = jax.ShapeDtypeStruct
    dec = shape((2 * len(TYPES), BLOCK * 16, WIDE), BF)
    tables = (
        shape((4, 2 * nz, 2 * nz), BF),
        shape((4, 2 * nz, nz), BF),
        shape((2 * TAPS, 8, nz), F32),
        shape((32, 8, nz), F32),
        dec,
        dec,
    )
    slots = rows // 2 + HALO
    spots = rows // 2 + REACH2
    blocks = rows // 4
    early = (rows - 2 * MID - 2) // 2 // FIELD_GROUP * FIELD_GROUP
    prepared = pl.pallas_call(
        functools.partial(exchange, ny),
        out_shape=(shape(((rows + 2 * HALO) * ny, nz), F32), *tables, shape((3, early, 8, nz), F32)),
        in_specs=[hbm] * 4,
        out_specs=[vmem] * 8,
        scratch_shapes=[pltpu.SMEM((TAPS,), F32)] * 3
        + [pltpu.VMEM((4, blocks, 16, 2 * nz), BF), pltpu.VMEM((8, 2 * blocks, 8, nz), F32)]
        + [pltpu.SemaphoreType.DMA((2, CHUNKS))] * 4
        + [pltpu.SemaphoreType.DMA, pltpu.SemaphoreType.DMA((3,))],
        compiler_params=pltpu.CompilerParams(collective_id=0, has_side_effects=True, vmem_limit_bytes=LIMIT1),
        name="exchange",
    )(*(pltpu.with_memory_space_constraint(v, pltpu.HBM) for v in (even_taps, odd_taps, low_taps, flat)))
    wav, who = (pltpu.with_memory_space_constraint(v.T, pltpu.HBM) for v in (wavelets, pairs))
    return pl.pallas_call(
        functools.partial(kernel, ny),
        out_shape=shape((per_dev, rows // 2, ny // 2, nz // 2), F32),
        in_specs=[hbm] * 2 + [vmem] * 8,
        out_specs=vmem,
        scratch_shapes=[
            pltpu.SMEM(wav.shape, jnp.int32),
            pltpu.SMEM(who.shape, jnp.int32),
            pltpu.VMEM((4, slots // 2, 16, 2 * nz), BF),
            pltpu.VMEM((8, slots, 8, nz), F32),
            pltpu.VMEM((2, slots // 2 + 1, 16, 2 * nz), BF),
            pltpu.VMEM((KEYS, spots, 8, nz), F32),
            pltpu.VMEM((KEYS, spots // 2 + 2 * BLOCK, 16, 2 * nz), BF),
            pltpu.SMEM((KEYS + 1,), jnp.int32),
            pltpu.SemaphoreType.DMA((2,)),
        ]
        + [pltpu.VMEM((2, WIDE, 2 * nz), BF)] * PAIR_GROUP,
        compiler_params=pltpu.CompilerParams(vmem_limit_bytes=LIMIT2),
        name="scatter",
    )(wav, who, *prepared)


def solution(mesh):
    placed = (P(("groups", "space"), None, None), P(), P(), P(), P(), P())
    return jax.shard_map(
        shards,
        mesh=mesh,
        in_specs=placed,
        out_specs=P("wave", ("groups", "space"), None, None),
        check_vma=False,
    )
```
